32 devices in a mesh: seq: 4 (over y, x), fsdp: 8 (over z, core).
Axes of the slice: x: 2, y: 2, z: 4, core: 2. Of those that a mesh axis runs over, the one named last changes fastest.
Arguments:
- inputs: bfloat16 [8, 1024, 2048], P('fsdp', 'seq'), may hold values from -40 to 40
- cotangent: bfloat16 [8, 1024, 2048], P('fsdp', 'seq'), may hold values from -6 to 6
- segments: int32 [8, 1024], P('fsdp'), may hold values from 0 to 7, never falling along the last dimension, each value on 1 to 256 neighbouring positions
- valid: int32 [8, 1024], P('fsdp', 'seq'), may hold values from 0 to 1, as said below
- norm_attn: bfloat16 [2048], P('fsdp'), may hold values from 0.5 to 1.5
- query_weight: bfloat16 [2048, 2048], P('fsdp'), may hold values from -0.0625 to 0.0625
- w_key: bfloat16 [2048, 2048], P('fsdp'), may hold values from -0.0625 to 0.0625
- w_value: bfloat16 [2048, 2048], P('fsdp'), may hold values from -0.125 to 0.125
- w_out: bfloat16 [2048, 2048], P('fsdp'), may hold values from -0.5 to 0.5
- rel_bias: bfloat16 [32, 32], replicated, may hold values from -4 to 4
- norm_ff: bfloat16 [2048], P('fsdp'), may hold values from 0.5 to 1.5
- w_gate: bfloat16 [2048, 5120], P('fsdp'), may hold values from -0.125 to 0.125
- w_up: bfloat16 [2048, 5120], P('fsdp'), may hold values from -0.125 to 0.125
- w_down: bfloat16 [2048, 5120], P('fsdp'), may hold values from -0.078125 to 0.078125
Outputs:
- output: bfloat16 [8, 1024, 2048], P('fsdp', 'seq')
- grad_inputs: bfloat16 [8, 1024, 2048], P('fsdp', 'seq')
- grad_norm_attn: float32 [2048], P('fsdp')
- grad_query: float32 [2048, 2048], P('fsdp')
- grad_key: float32 [2048, 2048], P('fsdp')
- grad_value: float32 [2048, 2048], P('fsdp')
- grad_out: float32 [2048, 2048], P('fsdp')
- grad_rel_bias: float32 [32, 32], replicated
- grad_norm_ff: float32 [2048], P('fsdp')
- grad_gate: float32 [2048, 5120], P('fsdp')
- grad_up: float32 [2048, 5120], P('fsdp')
- grad_down: float32 [2048, 5120], P('fsdp')
- rms_stats: float32 [4], replicated
The draws below stay inside these ranges and needn't reach their ends.
Inputs may be any that keep to these rules, and one draw needn't show every extreme that they name: `segments`: segment numbers never fall along a sequence; a document has 1 to 256 tokens, and some document of each sequence has exactly that many. In each sequence the valid tokens are a prefix; the prefixes of the 8 sequences have the lengths 1024 // 4**k, k = 0 to 7, in some order.
All inputs are finite; a program needn't handle non-finite values.
Results may differ from the reference program's by a relative error of at most 0.02.
Values may be sent and summed in bfloat16 or wider, within the bound.
No kernel may reach another device: no remote copies, remote signals or barrier semaphores. Data moves between devices by JAX's collectives and lax.ppermute only.
A program may use at most 384 MiB of HBM per device.

```python
import math
import jax
import jax.numpy as jnp
import numpy as np
from jax import lax

D = 2048
H = 32
DH = 64
FF = 5120
BUCKETS = 32
BATCH = 8
LENGTH = 1024


def draw_inputs(key, part):
    key_base, key_seq, key_tok, key_column_index = jax.random.split(key, 4)
    seq_scale = jnp.exp(jax.random.uniform(key_seq, (BATCH, 1, 1), jnp.float32, math.log(0.25), math.log(4.0)))
    tok_scale = jnp.exp(jax.random.uniform(key_tok, (BATCH, LENGTH, 1), jnp.float32, math.log(0.7), math.log(1.4)))
    col_scale = jnp.exp(jax.random.uniform(key_column_index, (1, 1, D), jnp.float32, math.log(0.5), math.log(2.0)))
    raw_values = jnp.clip(jax.random.normal(key_base, (BATCH, LENGTH, D), jnp.float32), -3.5, 3.5)
    return (raw_values * seq_scale * tok_scale * col_scale).astype(jnp.bfloat16)


def draw_valid(key, part):
    ranking = jax.random.permutation(key, BATCH).astype(jnp.int32)
    shift_bits = jnp.minimum(2 * ranking, 30).astype(jnp.int32)
    prefix_len = (LENGTH // jnp.left_shift(jnp.ones_like(shift_bits), shift_bits)).astype(jnp.int32)
    return (jnp.arange(LENGTH, dtype=jnp.int32)[None, :] < prefix_len[:, None]).astype(jnp.int32)


def levels(rng, dims, cuts, low, largest):
    def one(axis_at, blocks):
        steps = jax.random.uniform(jax.random.fold_in(jax.random.fold_in(rng, 6), axis_at), (blocks,), jnp.float32, low / len(cuts), largest / len(cuts))
        return jnp.repeat(jnp.exp(steps), dims[axis_at] // blocks).reshape((-1,) + (1,) * (len(dims) - axis_at - 1))

    loudness = one(*cuts[0])
    for cut in cuts[1:]:
        loudness = loudness * one(*cut)
    return loudness


def length_profile(count, total, reach, lean):
    weights = [(1 << 20) // math.isqrt(grade ** lean) + 1 for grade in range(2, count + 1)]
    spare, counts = total - reach - (count - 1), [1] * (count - 1)
    while spare > 0:
        movable = [i for i in range(count - 1) if counts[i] < reach]
        mass, budget = sum([weights[i] for i in movable]), spare
        for i in movable:
            extra = min(reach - counts[i], max(1, budget * weights[i] // mass), spare)
            counts[i] = counts[i] + extra
            spare = spare - extra
    return np.array([reach] + counts)


def uneven(own_key, number_of, total, limit, skew):
    if number_of == 2:
        one = jax.random.randint(own_key, (), max(1, total - limit), min(limit, total - 1) + 1)
        return jnp.stack([one, total - one])
    lengths = jnp.asarray(length_profile(number_of, total, limit, skew), jnp.int32)
    pairs = (number_of - 1) // 2
    donor, receiver = lengths[1:1 + 2 * pairs:2], lengths[2:2 + 2 * pairs:2]
    margin = jnp.minimum(donor - 1, limit - receiver)
    shifted = jax.random.randint(jax.random.fold_in(own_key, 1), (pairs,), 0, 1 << 20) % (margin + 1)
    lengths = lengths.at[1:1 + 2 * pairs:2].set(donor - shifted).at[2:2 + 2 * pairs:2].set(receiver + shifted)
    return lengths[jax.random.permutation(jax.random.fold_in(own_key, 2), number_of)]


def centred(key, shape, width, reach, cuts=(), kind=jnp.bfloat16):
    gain = levels(key, shape, cuts, -0.22, 0.18) if cuts else 1.0
    drawn = jax.random.normal(key, shape, jnp.float32) * width * gain
    return jnp.minimum(jnp.maximum(drawn, -reach), reach).astype(kind)


def setup_inputs(seed: int = 0) -> dict:
    streams_of = jax.random.split(jax.random.key(seed), 15)
    return {
        "inputs": draw_inputs(jax.random.fold_in(streams_of[14], 71), 0),
        "cotangent": centred(streams_of[1], (BATCH, LENGTH, D), 1.0, 6.0, ((0, 8), (1, 4))),
        "segments": jax.vmap(lambda own: jnp.searchsorted(jnp.cumsum(uneven(own, 8, LENGTH, LENGTH // 4, 1)), jnp.arange(LENGTH), side="right"))(jax.random.split(streams_of[2], BATCH)).reshape((BATCH, LENGTH)).astype(jnp.int32),
        "valid": draw_valid(jax.random.fold_in(streams_of[14], 71), 0),
        "norm_attn": jnp.clip(1.0 + 0.1 * jax.random.normal(streams_of[4], (D,), jnp.float32), 0.5, 1.5).astype(jnp.bfloat16),
        "query_weight": centred(streams_of[5], (D, D), (4 * D) ** -0.5, 0.0625, ((0, 8),)),
        "w_key": centred(streams_of[6], (D, D), (4 * D) ** -0.5, 0.0625, ((0, 8),)),
        "w_value": centred(streams_of[7], (D, D), D ** -0.5, 0.125, ((0, 8),)),
        "w_out": centred(streams_of[8], (D, D), (D // 16) ** -0.5, 0.5, ((0, 8),)),
        "rel_bias": centred(streams_of[9], (BUCKETS, H), 1.0, 4.0),
        "norm_ff": jnp.clip(1.0 + 0.1 * jax.random.normal(streams_of[10], (D,), jnp.float32), 0.5, 1.5).astype(jnp.bfloat16),
        "w_gate": centred(streams_of[11], (D, FF), D ** -0.5, 0.125, ((0, 8),)),
        "w_up": centred(streams_of[12], (D, FF), D ** -0.5, 0.125, ((0, 8),)),
        "w_down": centred(streams_of[13], (D, FF), FF ** -0.5, 0.078125, ((0, 8),)),
    }


@jax.custom_vjp
def low(v):
    return lax.optimization_barrier(v.astype(jnp.bfloat16)).astype(jnp.float32)

@jax.custom_vjp
def low_back(v):
    return v

def low_keep(v):
    return (low(v), None)

def low_pass(kept, grad):
    return (grad,)

def back_keep(v):
    return (v, None)

def back_low(kept, grad):
    return (low(grad),)
low.defvjp(low_keep, low_pass)
low_back.defvjp(back_keep, back_low)
epsilon = 1e-06
masked_score = -1e+30
far_steps = (12, 16, 23, 32, 46, 64, 91)
highest = lax.Precision.HIGHEST

def bucket_of(relative):
    distance = jnp.abs(relative)
    far_bucket = jnp.full(relative.shape, 8, jnp.int32)
    for threshold in far_steps:
        far_bucket = far_bucket + (distance >= threshold).astype(jnp.int32)
    near_bucket = jnp.where(distance < 8, distance, far_bucket)
    return near_bucket + 16 * (relative > 0).astype(jnp.int32)

def attend_block(block_query, key_rows, value_rows, table, seg_row, first_row):
    row_count = block_query.shape[0]
    query_pos = first_row + jnp.arange(row_count, dtype=jnp.int32)
    key_pos = jnp.arange(key_rows.shape[0], dtype=jnp.int32)
    labels = bucket_of(key_pos[None, :] - query_pos[:, None])
    bias_rows = jnp.transpose(jnp.take(table, labels, axis=0), (2, 0, 1))
    scores = jnp.einsum('qhd,khd->hqk', block_query, key_rows, precision=highest) + bias_rows
    scores = low_back(scores)
    same_doc = lax.dynamic_slice_in_dim(seg_row, first_row, row_count)[:, None] == seg_row[None, :]
    scores = jnp.where(same_doc[None, :, :], scores, masked_score)
    top_score = lax.optimization_barrier(jnp.max(scores, axis=-1, keepdims=True))
    expo_scores = jnp.exp(scores - top_score)
    weights = low(expo_scores / lax.optimization_barrier(jnp.sum(expo_scores, axis=-1, keepdims=True)))
    return jnp.einsum('hqk,khd->qhd', weights, value_rows, precision=highest)

def encoder_layer(x_in, gain_one, query_weight, w_key, w_value, w_out, table, gain_two, w_gate, w_up, w_down, seg_rows):
    scale_one = lax.rsqrt(lax.optimization_barrier(jnp.mean(x_in * x_in, axis=-1, keepdims=True)) + epsilon)
    normed_one = low(x_in * scale_one * gain_one)
    queries = low_back(low(jnp.einsum('bld,de->ble', normed_one, query_weight, precision=highest)))
    key_proj = low_back(low(jnp.einsum('bld,de->ble', normed_one, w_key, precision=highest)))
    value_proj = low_back(low(jnp.einsum('bld,de->ble', normed_one, w_value, precision=highest)))
    head_shape = (BATCH, LENGTH, H, DH)
    block_rows = min(512, LENGTH)
    block_count = LENGTH // block_rows

    def one_sequence(element):
        seq_query, seq_key, sequence_value_rows, seg_row = element
        query_blocks = seq_query.reshape(block_count, block_rows, H, DH)
        block_starts = block_rows * jnp.arange(block_count, dtype=jnp.int32)

        def one_block(block_pair):
            return attend_block(block_pair[0], seq_key, sequence_value_rows, table, seg_row, block_pair[1])
        return lax.map(jax.checkpoint(one_block), (query_blocks, block_starts)).reshape(LENGTH, H * DH)
    context = lax.map(one_sequence, (queries.reshape(head_shape), key_proj.reshape(head_shape), value_proj.reshape(head_shape), seg_rows))
    context = low_back(low(context))
    attn_out = low_back(jnp.einsum('blc,oc->blo', context, w_out, precision=highest))
    middle = x_in + attn_out
    scale_two = lax.rsqrt(lax.optimization_barrier(jnp.mean(middle * middle, axis=-1, keepdims=True)) + epsilon)
    normed_two = low(middle * scale_two * gain_two)
    gate = low_back(jnp.einsum('bld,df->blf', normed_two, w_gate, precision=highest))
    up_proj = low_back(jnp.einsum('bld,df->blf', normed_two, w_up, precision=highest))
    hidden = low(jax.nn.gelu(gate, approximate=True) * up_proj)
    ff_out = jnp.einsum('blf,of->blo', hidden, w_down, precision=highest)
    return (middle + ff_out, (attn_out, middle, ff_out))

def reference(inputs, cotangent, segments, valid, norm_attn, query_weight, w_key, w_value, w_out, rel_bias, norm_ff, w_gate, w_up, w_down):

    def widen(array):
        return array.astype(jnp.float32)

    def forward(x_in, gain_one, wq_in, wk_in, wv_in, wo_in, table, gain_two, wg_in, wu_in, wd_in):
        return encoder_layer(x_in, gain_one, wq_in, wk_in, wv_in, wo_in, table, gain_two, wg_in, wu_in, wd_in, segments)
    primal, back_fn, extras = jax.vjp(forward, widen(inputs), widen(norm_attn), widen(query_weight), widen(w_key), widen(w_value), widen(w_out), widen(rel_bias), widen(norm_ff), widen(w_gate), widen(w_up), widen(w_down), has_aux=True)
    grads = back_fn(widen(cotangent))
    attn_out, middle, ff_out = extras
    live_mask = valid.astype(jnp.float32)[:, :, None]
    live_count = jnp.sum(live_mask) * D

    def root_mean(value_vectors):
        return jnp.sqrt(jnp.sum(live_mask * value_vectors * value_vectors) / live_count)
    rms_stats = jnp.stack([root_mean(widen(inputs)), root_mean(attn_out), root_mean(middle), root_mean(ff_out)])
    return (primal.astype(jnp.bfloat16), grads[0].astype(jnp.bfloat16), grads[1], grads[2], grads[3], grads[4], grads[5], grads[6], grads[7], grads[8], grads[9], grads[10], rms_stats)
```

```python
import jax
import jax.numpy as jnp
from jax import lax
from jax.experimental import pallas as pl
from jax.experimental.pallas import tpu as pltpu
from jax.sharding import PartitionSpec as P

DH = 64
LANES = 128
BLOCK = 128
NEAR = 3 * BLOCK
PAD = 2 * BLOCK

epsilon = 1e-06
masked_score = -1e30
far_steps = (12, 16, 23, 32, 46, 64, 91)
FAR_BUCKET = 8 + len(far_steps)

bf16 = jnp.bfloat16
f32 = jnp.float32


def bucket_of(relative):
    distance = jnp.abs(relative)
    far_bucket = jnp.full(relative.shape, 8, jnp.int32)
    for threshold in far_steps:
        far_bucket = far_bucket + (distance >= threshold).astype(jnp.int32)
    near_bucket = jnp.where(distance < 8, distance, far_bucket)
    return near_bucket + 16 * (relative > 0).astype(jnp.int32)


def near_onehot(buckets):
    key_pos = jnp.arange(NEAR, dtype=jnp.int32) - BLOCK
    query_pos = jnp.arange(BLOCK, dtype=jnp.int32)
    labels = bucket_of(key_pos[:, None] - query_pos[None, :])
    return labels[:, :, None] == jnp.arange(buckets, dtype=jnp.int32)


def swap(value, distance):
    return lax.ppermute(value, "seq", [(rank, rank ^ distance) for rank in range(4)])


def seq_gather(own):
    half = own.shape[0] // 2
    one, two = swap(own, 1), swap(own, 2)
    return [own, one, two, swap(one[:half], 2), swap(two[half:], 1)]


def seq_scatter_sum(rows):
    count = rows.shape[0] // 4
    half = count // 2

    def piece(chunk, second):
        start = chunk * count + second * half
        return rows[start : start + half]

    def add(left, right):
        return left.astype(f32) + right.astype(f32)

    got_one = swap(jnp.concatenate([piece(3, 0), piece(1, 0)]), 1)
    got_two = swap(jnp.concatenate([piece(3, 1), piece(2, 1)]), 2)
    first_out = add(piece(2, 0), got_one[:half]).astype(bf16)
    second_out = add(piece(1, 1), got_two[:half]).astype(bf16)
    first_in = swap(first_out, 2)
    second_in = swap(second_out, 1)
    first = add(add(piece(0, 0), got_one[half:]), first_in)
    second = add(add(piece(0, 1), got_two[half:]), second_in)
    return jnp.concatenate([first, second])


def sum_everywhere(value, axis_sizes):
    for name, size in axis_sizes:
        step = 1
        while step < size:
            value = value + lax.ppermute(value, name, [(i, i ^ step) for i in range(size)])
            step *= 2
    return value


def column_pick(rank, arrays, build, out_widths, parts):
    rows = arrays[0].shape[0]
    width = [a.shape[1] // parts for a in arrays]
    return pl.pallas_call(
        build,
        out_shape=[jax.ShapeDtypeStruct((rows, w), bf16) for w in out_widths],
        grid_spec=pltpu.PrefetchScalarGridSpec(
            num_scalar_prefetch=1,
            grid=(1,),
            in_specs=[pl.BlockSpec((rows, w), lambda i, r: (0, r[0])) for w in width],
            out_specs=[pl.BlockSpec((rows, w), lambda i, r: (0, 0)) for w in out_widths],
        ),
        name="column_pick",
    )(rank, *arrays)


def pick_attention(rank_ref, q_ref, k_ref, v_ref, o_ref, out_ref):
    width = q_ref.shape[1]
    for pair in range(width // LANES):
        for which, ref in enumerate((q_ref, k_ref, v_ref)):
            start = (3 * pair + which) * LANES
            out_ref[:, start : start + LANES] = ref[:, pair * LANES : (pair + 1) * LANES]
    out_ref[:, 3 * width :] = o_ref[...]


def pick_hidden(rank_ref, g_ref, u_ref, d_ref, gu_ref, down_ref):
    width = g_ref.shape[1]
    gu_ref[:, :width] = g_ref[...]
    gu_ref[:, width:] = u_ref[...]
    down_ref[...] = d_ref[...]


def column_place(rank, pieces, out_count, store):
    rows, width = pieces[0].shape
    half = rows // 2
    out_width = width // out_count

    def body(rank_ref, own_ref, one_ref, two_ref, lo_ref, hi_ref, *out_refs):
        distance = pl.program_id(0) ^ rank_ref[0]
        for index, ref in enumerate((own_ref, one_ref, two_ref)):

            @pl.when(distance == index)
            def _(ref=ref):
                store(ref, out_refs, slice(0, rows))

        @pl.when(distance == 3)
        def _():
            store(lo_ref, out_refs, slice(0, half))
            store(hi_ref, out_refs, slice(half, rows))

    return pl.pallas_call(
        body,
        out_shape=[jax.ShapeDtypeStruct((rows, 4 * out_width), f32)] * out_count,
        grid_spec=pltpu.PrefetchScalarGridSpec(
            num_scalar_prefetch=1,
            grid=(4,),
            in_specs=[pl.BlockSpec(p.shape, lambda q, r: (0, 0)) for p in pieces],
            out_specs=[pl.BlockSpec((rows, out_width), lambda q, r: (0, q))] * out_count,
        ),
        name="column_place",
    )(rank, *pieces)


def store_plain(ref, out_refs, rows):
    width = out_refs[0].shape[1]
    for index, out in enumerate(out_refs):
        out[rows, :] = ref[:, index * width : (index + 1) * width].astype(f32)


def store_pairs(ref, out_refs, rows):
    for pair in range(out_refs[0].shape[1] // LANES):
        for which, out in enumerate(out_refs):
            start = (3 * pair + which) * LANES
            out[rows, pair * LANES : (pair + 1) * LANES] = ref[:, start : start + LANES].astype(f32)


def matmul_nt(left, right):
    return lax.dot_general(
        left, right, (((1,), (1,)), ((), ())), preferred_element_type=f32
    )


def matmul_nn(left, right):
    return jnp.dot(left, right, preferred_element_type=f32)


def two_heads(rows):
    lane = lax.broadcasted_iota(jnp.int32, rows.shape, 1)
    none = jnp.zeros_like(rows)
    return jnp.concatenate(
        [jnp.where(lane < DH, rows, none), jnp.where(lane < DH, none, rows)], axis=0
    )


def one_pair(columns):
    count = columns.shape[1] // 2
    left, right = columns[:, :count], columns[:, count:]
    row = lax.broadcasted_iota(jnp.int32, left.shape, 0)
    return jnp.where(row < DH, left, right).T


def held_at(rank_ref, block, per_chunk):
    chunk = (block // per_chunk) ^ rank_ref[0]
    return pl.multiple_of((chunk * per_chunk + block % per_chunk) * BLOCK, BLOCK)


def far_is_live(seg_ref, block, blocks, side):
    other = block + 2 * side
    inside = jnp.logical_and(other >= 0, other < blocks)
    other = jnp.clip(other, 0, blocks - 1)
    if side < 0:
        same = seg_ref[other * BLOCK + BLOCK - 1] == seg_ref[block * BLOCK]
    else:
        same = seg_ref[other * BLOCK] == seg_ref[block * BLOCK + BLOCK - 1]
    return jnp.logical_and(inside, same)


def forward_kernel(
    rank_ref, seg_ref, qkv_ref, bias_ref, far_ref, key_seg_ref, query_seg_ref,
    out_ref, log_ref, k_ref, vt_ref, top_ref, total_ref, acc_ref, *, per_chunk,
):
    length = qkv_ref.shape[0]
    blocks = length // BLOCK
    for edge in (0, PAD + length):
        k_ref[edge : edge + PAD, :] = jnp.zeros((PAD, LANES), bf16)
        vt_ref[:, edge : edge + PAD] = jnp.zeros((LANES, PAD), bf16)
    for block in range(blocks):
        row = held_at(rank_ref, block, per_chunk)
        start = PAD + block * BLOCK
        k_ref[start : start + BLOCK, :] = qkv_ref[pl.ds(row, BLOCK), LANES : 2 * LANES]
        vt_ref[:, start : start + BLOCK] = qkv_ref[pl.ds(row, BLOCK), 2 * LANES :].T

    def one_block(block, carry):
        row = held_at(rank_ref, block, per_chunk)
        query = two_heads(qkv_ref[pl.ds(row, BLOCK), :LANES])
        query_seg = query_seg_ref[pl.ds(block, 1), :]

        def scores_at(start, count, bias):
            scores = matmul_nt(k_ref[pl.ds(start, count), :], query) + bias
            key_seg = key_seg_ref[pl.ds(start, count), :]
            same = jnp.concatenate([key_seg, key_seg], axis=1) == query_seg
            return jnp.where(same, scores, masked_score)

        start = pl.multiple_of(PAD - BLOCK + block * BLOCK, BLOCK)
        scores = scores_at(start, NEAR, bias_ref[0])
        top = jnp.max(scores, axis=0, keepdims=True)
        expo = jnp.exp(scores - top)
        top_ref[...] = top
        total_ref[...] = jnp.sum(expo, axis=0, keepdims=True)
        acc_ref[...] = matmul_nn(vt_ref[:, pl.ds(start, NEAR)], expo.astype(bf16))

        for index, side in enumerate((-1, 1)):

            @pl.when(far_is_live(seg_ref, block, blocks, side))
            def _(index=index, side=side):
                start = pl.multiple_of(PAD + (block + 2 * side) * BLOCK, BLOCK)
                scores = scores_at(start, BLOCK, far_ref[0, index : index + 1, :])
                old_top = top_ref[...]
                top = jnp.maximum(old_top, jnp.max(scores, axis=0, keepdims=True))
                scale = jnp.exp(old_top - top)
                expo = jnp.exp(scores - top)
                top_ref[...] = top
                total_ref[...] = total_ref[...] * scale + jnp.sum(expo, axis=0, keepdims=True)
                acc_ref[...] = acc_ref[...] * scale + matmul_nn(
                    vt_ref[:, pl.ds(start, BLOCK)], expo.astype(bf16)
                )

        total = total_ref[...]
        out_ref[pl.ds(row, BLOCK), :] = one_pair(acc_ref[...] / total).astype(bf16)
        log_ref[0, pl.ds(block, 1), :] = top_ref[...] + jnp.log(total)
        return carry

    lax.fori_loop(0, blocks, one_block, 0)


def backward_kernel(
    rank_ref, seg_ref, qkv_ref, out_ref, dout_ref, log_ref, bias_ref, far_ref, key_seg_ref,
    query_seg_ref, grad_ref, near_grad_ref, far_grad_ref,
    k_ref, kt_ref, v_ref, dk_ref, dv_ref, dq_ref, *, per_chunk,
):
    length = qkv_ref.shape[0]
    blocks = length // BLOCK
    for edge in (0, PAD + length):
        k_ref[edge : edge + PAD, :] = jnp.zeros((PAD, LANES), bf16)
        kt_ref[:, edge : edge + PAD] = jnp.zeros((LANES, PAD), bf16)
        v_ref[edge : edge + PAD, :] = jnp.zeros((PAD, LANES), bf16)
    for block in range(blocks):
        row = held_at(rank_ref, block, per_chunk)
        start = PAD + block * BLOCK
        key = qkv_ref[pl.ds(row, BLOCK), LANES : 2 * LANES]
        k_ref[start : start + BLOCK, :] = key
        kt_ref[:, start : start + BLOCK] = key.T
        v_ref[start : start + BLOCK, :] = qkv_ref[pl.ds(row, BLOCK), 2 * LANES :]
    dk_ref[...] = jnp.zeros_like(dk_ref)
    dv_ref[...] = jnp.zeros_like(dv_ref)
    near_grad_ref[...] = jnp.zeros_like(near_grad_ref)
    far_grad_ref[...] = jnp.zeros_like(far_grad_ref)

    def one_block(block, carry):
        row = held_at(rank_ref, block, per_chunk)
        query = two_heads(qkv_ref[pl.ds(row, BLOCK), :LANES])
        dout_rows = dout_ref[pl.ds(row, BLOCK), :]
        dout = two_heads(dout_rows)
        query_seg = query_seg_ref[pl.ds(block, 1), :]
        log_row = log_ref[0, pl.ds(block, 1), :]
        product = (dout_rows.astype(f32) * out_ref[pl.ds(row, BLOCK), :].astype(f32)).T
        row_dot = jnp.concatenate(
            [
                jnp.sum(product[:DH], axis=0, keepdims=True),
                jnp.sum(product[DH:], axis=0, keepdims=True),
            ],
            axis=1,
        )

        def d_scores_at(start, count, bias):
            scores = matmul_nt(k_ref[pl.ds(start, count), :], query) + bias
            key_seg = key_seg_ref[pl.ds(start, count), :]
            same = jnp.concatenate([key_seg, key_seg], axis=1) == query_seg
            prob = jnp.exp(jnp.where(same, scores, masked_score) - log_row)
            d_prob = matmul_nt(v_ref[pl.ds(start, count), :], dout)
            d_scores = prob * (d_prob - row_dot)
            low = d_scores.astype(bf16)
            dk_ref[pl.ds(start, count), :] += matmul_nn(low, query)
            dv_ref[pl.ds(start, count), :] += matmul_nn(prob.astype(bf16), dout)
            return d_scores, matmul_nn(kt_ref[:, pl.ds(start, count)], low)

        start = pl.multiple_of(PAD - BLOCK + block * BLOCK, BLOCK)
        d_scores, d_query = d_scores_at(start, NEAR, bias_ref[0])
        near_grad_ref[0] += d_scores
        dq_ref[...] = d_query
        for index, side in enumerate((-1, 1)):

            @pl.when(far_is_live(seg_ref, block, blocks, side))
            def _(index=index, side=side):
                start = pl.multiple_of(PAD + (block + 2 * side) * BLOCK, BLOCK)
                d_scores, d_query = d_scores_at(start, BLOCK, far_ref[0, index : index + 1, :])
                far_grad_ref[0, index : index + 1, :] += jnp.sum(d_scores, axis=0, keepdims=True)
                dq_ref[...] += d_query

        grad_ref[pl.ds(row, BLOCK), :LANES] = one_pair(dq_ref[...]).astype(bf16)
        return carry

    lax.fori_loop(0, blocks, one_block, 0)
    for block in range(blocks):
        row = held_at(rank_ref, block, per_chunk)
        start = PAD + block * BLOCK
        grad_ref[pl.ds(row, BLOCK), LANES : 2 * LANES] = dk_ref[start : start + BLOCK, :].astype(bf16)
        grad_ref[pl.ds(row, BLOCK), 2 * LANES :] = dv_ref[start : start + BLOCK, :].astype(bf16)


def attention_specs(length, blocks):
    whole = lambda p, *_: (0, 0)
    return {
        "qkv": pl.BlockSpec((length, 3 * LANES), lambda p, *_: (0, p)),
        "head": pl.BlockSpec((length, LANES), lambda p, *_: (0, p)),
        "log": pl.BlockSpec((1, blocks, 2 * BLOCK), lambda p, *_: (p, 0, 0)),
        "bias": pl.BlockSpec((1, NEAR, 2 * BLOCK), lambda p, *_: (p, 0, 0)),
        "far": pl.BlockSpec((1, 8, 2 * BLOCK), lambda p, *_: (p, 0, 0)),
        "key_seg": pl.BlockSpec((length + 2 * PAD, LANES), whole),
        "query_seg": pl.BlockSpec((blocks, 2 * BLOCK), whole),
    }


def attention_forward(rank, seg_row, qkv, bias):
    length = qkv.shape[0]
    blocks, pairs = length // BLOCK, qkv.shape[1] // (3 * LANES)
    spec = attention_specs(length, blocks)
    padded = (length + 2 * PAD, LANES)

    def body(*refs):
        forward_kernel(*refs, per_chunk=blocks // 4)

    return pl.pallas_call(
        body,
        out_shape=[
            jax.ShapeDtypeStruct((length, pairs * LANES), bf16),
            jax.ShapeDtypeStruct((pairs, blocks, 2 * BLOCK), f32),
        ],
        grid_spec=pltpu.PrefetchScalarGridSpec(
            num_scalar_prefetch=2,
            grid=(pairs,),
            in_specs=[spec[n] for n in ("qkv", "bias", "far", "key_seg", "query_seg")],
            out_specs=[spec["head"], spec["log"]],
            scratch_shapes=[
                pltpu.VMEM(padded, bf16),
                pltpu.VMEM(padded[::-1], bf16),
                pltpu.VMEM((1, 2 * BLOCK), f32),
                pltpu.VMEM((1, 2 * BLOCK), f32),
                pltpu.VMEM((LANES, 2 * BLOCK), f32),
            ],
        ),
        name="attention_forward",
    )(rank, seg_row, qkv, *bias)


def attention_backward(rank, seg_row, qkv, context, d_context, logs, bias):
    length = qkv.shape[0]
    blocks, pairs = length // BLOCK, qkv.shape[1] // (3 * LANES)
    spec = attention_specs(length, blocks)
    padded = (length + 2 * PAD, LANES)

    def body(*refs):
        backward_kernel(*refs, per_chunk=blocks // 4)

    names = ("qkv", "head", "head", "log", "bias", "far", "key_seg", "query_seg")
    return pl.pallas_call(
        body,
        out_shape=[
            jax.ShapeDtypeStruct(qkv.shape, bf16),
            jax.ShapeDtypeStruct((pairs, NEAR, 2 * BLOCK), f32),
            jax.ShapeDtypeStruct((pairs, 8, 2 * BLOCK), f32),
        ],
        grid_spec=pltpu.PrefetchScalarGridSpec(
            num_scalar_prefetch=2,
            grid=(pairs,),
            in_specs=[spec[n] for n in names],
            out_specs=[spec["qkv"], spec["bias"], spec["far"]],
            scratch_shapes=[
                pltpu.VMEM(padded, bf16),
                pltpu.VMEM(padded[::-1], bf16),
                pltpu.VMEM(padded, bf16),
                pltpu.VMEM(padded, f32),
                pltpu.VMEM(padded, f32),
                pltpu.VMEM((LANES, 2 * BLOCK), f32),
            ],
        ),
        name="attention_backward",
    )(rank, seg_row, qkv, context, d_context, logs, *bias)


def bias_operands(table, seg_row):
    buckets, heads = table.shape
    pairs = heads // 2
    near = jnp.einsum(
        "jik,kh->hji", near_onehot(buckets).astype(bf16), table, preferred_element_type=f32
    )
    near = near.reshape(pairs, 2, NEAR, BLOCK).transpose(0, 2, 1, 3).reshape(pairs, NEAR, 2 * BLOCK)
    ends = jnp.stack([table[FAR_BUCKET], table[FAR_BUCKET + 16]]).astype(f32)
    ends = ends.reshape(2, pairs, 2).transpose(1, 0, 2)
    far = jnp.broadcast_to(ends[:, :, :, None], (pairs, 2, 2, BLOCK)).reshape(pairs, 2, 2 * BLOCK)
    far = jnp.pad(far, ((0, 0), (0, 6), (0, 0)))
    key_seg = jnp.broadcast_to(
        jnp.pad(seg_row, (PAD, PAD), constant_values=-1)[:, None], (seg_row.shape[0] + 2 * PAD, LANES)
    )
    rows = seg_row.reshape(-1, BLOCK)
    return near, far, key_seg, jnp.concatenate([rows, rows], axis=1)


def table_grad(near_grad, far_grad, buckets):
    pairs = near_grad.shape[0]
    near = near_grad.reshape(pairs, NEAR, 2, BLOCK)
    table = jnp.einsum(
        "pjhi,jik->kph", near, near_onehot(buckets).astype(f32), precision=lax.Precision.HIGHEST
    ).reshape(buckets, 2 * pairs)
    far = jnp.sum(far_grad.reshape(pairs, 8, 2, BLOCK), axis=-1)
    for index, bucket in enumerate((FAR_BUCKET, FAR_BUCKET + 16)):
        table = table.at[bucket].add(far[:, index].reshape(2 * pairs))
    return table


def tanh_parts(gate):
    inner = 0.7978845608028654 * (gate + 0.044715 * gate * gate * gate)
    slope = 0.7978845608028654 * (1.0 + 3.0 * 0.044715 * gate * gate)
    return jnp.tanh(inner), slope


def on_device(
    inputs,
    cotangent,
    segments,
    valid,
    norm_attn,
    query_weight,
    w_key,
    w_value,
    w_out,
    rel_bias,
    norm_ff,
    w_gate,
    w_up,
    w_down,
    *,
    axis_sizes,
):
    seq_index = lax.axis_index("seq")
    rank = seq_index.reshape(1).astype(jnp.int32)
    shard_rows, model_width = query_weight.shape
    hidden_units = w_gate.shape[1]
    parts = dict(axis_sizes)["seq"]
    attn_part = model_width // parts
    hidden_part = hidden_units // parts
    heads_local = attn_part // DH
    seg_row = segments[0]
    x_low, grad_low = inputs[0], cotangent[0]
    x_in = x_low.astype(f32)

    (attn_own,) = column_pick(
        rank, (query_weight, w_key, w_value, w_out), pick_attention, (4 * attn_part,), parts
    )
    attn_weight = lax.all_gather(attn_own, "fsdp", axis=0, tiled=True)
    gu_own, down_own = column_pick(
        rank, (w_gate, w_up, w_down), pick_hidden, (2 * hidden_part, hidden_part), parts
    )
    gu_weight = lax.all_gather(gu_own, "fsdp", axis=0, tiled=True)
    down_weight = lax.all_gather(down_own, "fsdp", axis=0, tiled=True)
    gains = lax.all_gather(jnp.stack([norm_attn, norm_ff]), "fsdp", axis=1, tiled=True).astype(f32)
    gain_one, gain_two = gains[0:1], gains[1:2]
    qkv_weight, out_weight = attn_weight[:, : 3 * attn_part], attn_weight[:, 3 * attn_part :]

    def scale_of(rows):
        return lax.rsqrt(jnp.mean(rows * rows, axis=-1, keepdims=True) + epsilon)

    def gathered(own):
        return jnp.concatenate(seq_gather(own))

    def trans_dot(left_side, right_side):
        return lax.dot_general(
            left_side, right_side, (((0,), (0,)), ((), ())), preferred_element_type=f32
        ).astype(bf16)

    def over_shards(gradient):
        return lax.psum_scatter(gradient, "fsdp", scatter_dimension=0, tiled=True)

    x_all = gathered(x_low).astype(f32)
    normed_one = (x_all * scale_of(x_all) * gain_one).astype(bf16)
    table = lax.dynamic_slice_in_dim(rel_bias, seq_index * heads_local, heads_local, 1)
    bias = bias_operands(table, seg_row)
    qkv = jnp.dot(normed_one, qkv_weight, preferred_element_type=f32).astype(bf16)
    context, logs = attention_forward(rank, seg_row, qkv, bias)
    attn_out = seq_scatter_sum(matmul_nt(context, out_weight).astype(bf16))
    middle = x_in + attn_out
    scale_two = scale_of(middle)
    normed_two = gathered((middle * scale_two * gain_two).astype(bf16))
    grad_all = gathered(grad_low)
    gate_up = jnp.dot(normed_two, gu_weight, preferred_element_type=f32)
    gate, up_proj = gate_up[:, :hidden_part], gate_up[:, hidden_part:]
    bend, slope = tanh_parts(gate)
    act = 0.5 * gate * (1.0 + bend)
    hidden = lax.optimization_barrier((act * up_proj).astype(bf16))
    sum_down = over_shards(trans_dot(grad_all, hidden))
    ff_out = seq_scatter_sum(matmul_nt(hidden, down_weight).astype(bf16))
    output = (middle + ff_out).astype(bf16)[None]

    d_hidden = jnp.dot(grad_all, down_weight, preferred_element_type=f32)
    d_gate = d_hidden * up_proj * (0.5 * (1.0 + bend) + 0.5 * gate * (1.0 - bend * bend) * slope)
    d_gu = jnp.concatenate([d_gate.astype(bf16), (d_hidden * act).astype(bf16)], axis=1)
    d_normed_two = seq_scatter_sum(matmul_nt(d_gu, gu_weight).astype(bf16))
    sum_gu = over_shards(trans_dot(normed_two, d_gu))
    unit_two = d_normed_two * gain_two
    d_middle = (
        grad_low.astype(f32)
        + scale_two * unit_two
        - middle * scale_two**3 * jnp.mean(unit_two * middle, axis=-1, keepdims=True)
    )

    d_attn = gathered(d_middle.astype(bf16))
    d_context = jnp.dot(d_attn, out_weight, preferred_element_type=f32).astype(bf16)
    d_qkv, near_grad, far_grad = attention_backward(
        rank, seg_row, qkv, context, d_context, logs, bias
    )
    sum_qkv = over_shards(trans_dot(normed_one, d_qkv))
    sum_out = over_shards(trans_dot(d_attn, context))
    d_normed_one = seq_scatter_sum(matmul_nt(d_qkv, qkv_weight).astype(bf16))
    scale_one = scale_of(x_in)
    unit_one = d_normed_one * gain_one
    d_input = (
        d_middle
        + scale_one * unit_one
        - x_in * scale_one**3 * jnp.mean(unit_one * x_in, axis=-1, keepdims=True)
    )
    grad_inputs = d_input.astype(bf16)[None]

    (grad_down,) = column_place(rank, seq_gather(sum_down), 1, store_plain)
    grad_gate, grad_up = column_place(rank, seq_gather(sum_gu), 2, store_plain)
    (grad_out,) = column_place(rank, seq_gather(sum_out), 1, store_plain)
    grad_query, grad_key, grad_value = column_place(rank, seq_gather(sum_qkv), 3, store_pairs)

    def gain_grad(pairs, gain):
        total = sum(jnp.sum(weight.astype(f32) * grad, axis=1) for weight, grad in pairs)
        return total / gain.astype(f32)

    grad_norm_ff = gain_grad(((w_gate, grad_gate), (w_up, grad_up)), norm_ff)
    grad_norm_attn = gain_grad(
        ((query_weight, grad_query), (w_key, grad_key), (w_value, grad_value)), norm_attn
    )

    live_rows = valid[0].astype(f32)

    def live_sum(rows):
        return jnp.sum(live_rows * jnp.sum(rows * rows, axis=-1))

    stats = jnp.stack(
        [live_sum(x_in), live_sum(attn_out), live_sum(middle), live_sum(ff_out), jnp.sum(live_rows)]
    )
    d_table = table_grad(near_grad, far_grad, rel_bias.shape[0])
    table_full = lax.dynamic_update_slice_in_dim(
        jnp.zeros(rel_bias.shape, f32), d_table, seq_index * heads_local, 1
    )
    packed = jnp.concatenate([table_full, jnp.pad(stats, (0, table_full.shape[1] - 5))[None]])
    packed = sum_everywhere(packed, axis_sizes)
    table_sum, stat_sum = packed[:-1], packed[-1]
    rms_stats = jnp.sqrt(stat_sum[:4] / (stat_sum[4] * model_width))
    return (
        output,
        grad_inputs,
        grad_norm_attn,
        grad_query,
        grad_key,
        grad_value,
        grad_out,
        table_sum,
        grad_norm_ff,
        grad_gate,
        grad_up,
        grad_down,
        rms_stats,
    )


def solution(mesh):
    placed = (
        P("fsdp", "seq", None),
        P("fsdp", "seq", None),
        P("fsdp", None),
        P("fsdp", "seq"),
        P("fsdp"),
        P("fsdp", None),
        P("fsdp", None),
        P("fsdp", None),
        P("fsdp", None),
        P(),
        P("fsdp"),
        P("fsdp", None),
        P("fsdp", None),
        P("fsdp", None),
    )
    axis_sizes = tuple((name, mesh.shape[name]) for name in ("seq", "fsdp"))

    def body(*arrays):
        return on_device(*arrays, axis_sizes=axis_sizes)

    return jax.shard_map(
        body,
        mesh=mesh,
        in_specs=placed,
        out_specs=(
            P("fsdp", "seq", None),
            P("fsdp", "seq", None),
            P("fsdp"),
            P("fsdp", None),
            P("fsdp", None),
            P("fsdp", None),
            P("fsdp", None),
            P(),
            P("fsdp"),
            P("fsdp", None),
            P("fsdp", None),
            P("fsdp", None),
            P(),
        ),
        check_vma=False,
    )
```
